512 devices in a mesh: layer: 8 (over y, core), col: 64 (over x, z).
Axes of the slice: x: 4, y: 4, z: 16, core: 2. Of those that a mesh axis runs over, the one named last changes fastest.
Arguments:
- pivot_blocks: bfloat16 [8, 1024, 1024], P('layer'), may hold values from 0 to 6, as said below
- couplings: bfloat16 [8, 3072, 1024], P('layer', 'col'), may hold values from -0.1875 to 0.1875
- pattern: int32 [8, 12, 4], P('layer'), may hold values 0 or 1
- front_base: float32 [3072, 3072], P('col'), may hold values from -4 to 26, as said below
Outputs:
- panels: bfloat16 [8, 3072, 1024], P('layer', 'col')
- factor_rows: bfloat16 [2048, 1024], P('col')
- schur: float32 [2048, 2048], P('col', 'layer')
The draws below stay inside these ranges and needn't reach their ends.
Inputs may be any that keep to these rules, and one draw needn't show every extreme that they name: `pivot_blocks`: symmetric positive definite, with each diagonal entry between 4 and 6. `front_base`: symmetric positive definite, with each diagonal entry between 12 and 26.
All inputs are finite; a program needn't handle non-finite values. No bound on the sum of `pattern` on one device may be relied on, other than what follows from the above.
Results may differ from the reference program's by a relative error of at most 0.0039.
Values may be sent and summed in bfloat16 or wider, within the bound.
A program may use at most 128 MiB of HBM per device.

```python
import jax
import jax.numpy as jnp
import numpy as np
from jax import lax

R = 3072
P_SIZE = 1024
P2 = 1024
BLK = 256
N_LAYER = 8
N_COL = 64


def draw_pivot_blocks(key, part):
    first, second = jax.random.split(key)
    values = jax.random.uniform(first, (N_LAYER, P_SIZE, P_SIZE), jnp.float32, -1.0, 1.0)
    off = 0.1 + 0.02 * (values + jnp.swapaxes(values, 1, 2))
    diag = jax.random.uniform(second, (N_LAYER, P_SIZE), jnp.float32, 4.0, 6.0)
    eye = jnp.eye(P_SIZE, dtype=jnp.float32)
    return (off * (1.0 - eye) + diag[:, :, None] * eye).astype(jnp.bfloat16)


def draw_front_base(key, part):
    first, second = jax.random.split(jax.random.fold_in(key, 7))
    factor = jax.random.normal(first, (R, R), jnp.float32)
    factor = factor / R ** 0.5
    gram = 8.0 * jnp.dot(factor, factor.T, preferred_element_type=jnp.float32)
    gram = 0.5 * (gram + gram.T)
    diag = jax.random.uniform(second, (R,), jnp.float32, 8.0, 12.0)
    eye = jnp.eye(R, dtype=jnp.float32)
    return gram + diag[:, None] * eye + 0.5


def set_ends(result, stream_key, least, largest):
    longest = result.shape.index(max(result.shape))
    spots = []
    for shift in (0, 1):
        where = [jax.random.randint(jax.random.fold_in(stream_key, axis), (), 0, length) for axis, length in enumerate(result.shape)]
        where[longest] = (where[longest] + shift) % result.shape[longest]
        spots.append(tuple(where))
    return result.at[spots[0]].set(least).at[spots[1]].set(largest)


def levels(rng, dims, shards, least, high):
    factor_of, own = 1.0, jax.random.fold_in(rng, 6)
    for position, blocks in shards:
        heights = jnp.exp(jax.random.uniform(jax.random.fold_in(own, position), (blocks,), jnp.float32, least / len(shards), high / len(shards)))
        factor_of = factor_of * jnp.repeat(heights, dims[position] // blocks).reshape([-1 if axis == position else 1 for axis in range(len(dims))])
    return factor_of


def gaussian(rng, dims, deviation, most, shards=(), kind=jnp.bfloat16):
    array = jax.random.normal(rng, dims, jnp.float32) * deviation
    if len(shards) > 0:
        array = levels(rng, dims, shards, -0.22, 0.18) * array
    return jnp.clip(array, min=-most, max=most).astype(kind)


def setup_inputs(seed: int = 0) -> dict:
    streams_of = jax.random.split(jax.random.key(seed), 5)
    pivot_blocks = draw_pivot_blocks(jax.random.fold_in(streams_of[4], 71), 0)
    couplings = gaussian(streams_of[1], (N_LAYER, R, P_SIZE), P_SIZE ** -0.5, 0.1875, ((0, 8), (1, 64)))
    pattern = set_ends((jax.random.randint(streams_of[2], (N_LAYER, R // BLK, P_SIZE // BLK), 0, 4) < 3).astype(jnp.int32), jax.random.fold_in(streams_of[2], 1), 0, 1)
    front_base = draw_front_base(jax.random.fold_in(streams_of[4], 71), 0)
    return {"pivot_blocks": pivot_blocks, "couplings": couplings, "pattern": pattern, "front_base": front_base}


def block_cholesky(matrix):
    order = matrix.shape[0]
    if order <= 128:
        return jnp.linalg.cholesky(matrix)
    half = order // 2
    upper_left = block_cholesky(matrix[:half, :half])
    lower_left = jax.scipy.linalg.solve_triangular(upper_left, matrix[half:, :half].T, lower=True).T
    trailing = matrix[half:, half:] - jnp.dot(lower_left.astype(jnp.float32), lower_left.T.astype(jnp.float32), precision=lax.Precision.HIGHEST, preferred_element_type=jnp.float32)
    lower_right = block_cholesky(trailing)
    top_rows = jnp.concatenate([upper_left, jnp.zeros((half, order - half), matrix.dtype)], axis=1)
    bottom_rows = jnp.concatenate([lower_left, lower_right], axis=1)
    return jnp.concatenate([top_rows, bottom_rows], axis=0)

def reference(pivot_blocks, couplings, pattern, front_base):
    front_terms = jnp.zeros((R, R), jnp.float32)
    panel_list = []
    for layer_rank in range(N_LAYER):
        expand = jnp.repeat(jnp.repeat(pattern[layer_rank], BLK, axis=0), BLK, axis=1)
        masked = couplings[layer_rank] * expand.astype(jnp.bfloat16)
        lower = block_cholesky(pivot_blocks[layer_rank].astype(jnp.float32))
        panel = jax.scipy.linalg.solve_triangular(lower, masked.astype(jnp.float32).T, lower=True).T
        panel = panel.astype(jnp.bfloat16)
        panel_list.append(panel)
        front_terms = front_terms + lax.dot_general(panel.astype(jnp.float32), panel.astype(jnp.float32), (((1,), (1,)), ((), ())), preferred_element_type=jnp.float32)
    front = front_base - front_terms
    rows_dev = R // N_COL
    piv_dev = P2 // N_COL
    nonpiv = rows_dev - piv_dev
    group = nonpiv // N_LAYER
    piv = (np.arange(N_COL)[:, None] * rows_dev + np.arange(piv_dev)[None, :]).ravel().astype(np.int32)
    rows = (np.arange(N_COL)[:, None] * rows_dev + piv_dev + np.arange(nonpiv)[None, :]).ravel().astype(np.int32)
    cols = (np.arange(N_LAYER)[:, None, None] * group + np.arange(N_COL)[None, :, None] * rows_dev + np.arange(group)[None, None, :] + piv_dev).ravel().astype(np.int32)
    colpos = (np.arange(N_LAYER)[:, None, None] * group + np.arange(N_COL)[None, :, None] * nonpiv + np.arange(group)[None, None, :]).ravel().astype(np.int32)
    top = block_cholesky(front[piv][:, piv])
    factor_rows = jax.scipy.linalg.solve_triangular(top, front[rows][:, piv].T, lower=True).T.astype(jnp.bfloat16)
    chosen = factor_rows[colpos]
    update = lax.dot_general(factor_rows.astype(jnp.float32), chosen.astype(jnp.float32), (((1,), (1,)), ((), ())), preferred_element_type=jnp.float32)
    schur = front[rows][:, cols] - update
    return (jnp.stack(panel_list), factor_rows, schur)
```

```python
import jax
import jax.numpy as jnp
from jax import lax
from jax.experimental import pallas as pl
from jax.experimental.pallas import tpu as pltpu
from jax.sharding import Mesh, PartitionSpec as P

P2 = 1024
BLK = 256
NB = 128
F32 = jnp.float32
BF16 = jnp.bfloat16
NT = (((1,), (1,)), ((), ()))
NN = (((1,), (0,)), ((), ()))


def halves(x):
    hi = x.astype(BF16)
    return hi, (x - hi.astype(F32)).astype(BF16)


def dot(a, b, dims):
    return lax.dot_general(a, b, dims, preferred_element_type=F32)


def dot3(a, b, dims):
    return dot(a[0], b[0], dims) + dot(a[1], b[0], dims) + dot(a[0], b[1], dims)


def tree(terms):
    while len(terms) > 1:
        terms = [a + b for a, b in zip(terms[::2], terms[1::2])] + terms[len(terms) & ~1 :]
    return terms[0]


def small_factor(row, first):
    spread = [jnp.broadcast_to(row[:, first + j : first + j + 1], (8, 128)) for j in range(8)]
    s = {(i, j): jnp.broadcast_to(spread[j][i : i + 1, :], (8, 128)) for j in range(8) for i in range(j, 8)}
    x, t = {}, {}
    for j in range(8):
        r = lax.rsqrt(s[j, j])
        x[j, j] = r
        for m in range(j):
            x[j, m] = -r * t[j, m]
        low = {i: s[i, j] * r for i in range(j + 1, 8)}
        for m in range(j + 1, 8):
            for i in range(m, 8):
                s[i, m] = s[i, m] - low[i] * low[m]
        for i in range(j + 1, 8):
            for m in range(j + 1):
                term = low[i] * x[j, m]
                t[i, m] = t[i, m] + term if (i, m) in t else term
    return x


def inverse_factor(rows):
    lane = lax.broadcasted_iota(jnp.int32, (8, 128), 1)
    sub = lax.broadcasted_iota(jnp.int32, (8, 128), 0)
    zero = jnp.zeros((8, 128), F32)
    rows = list(rows)
    out = []
    for p in range(16):
        c0 = 8 * p
        x = small_factor(rows[p], c0)
        inside = jnp.logical_and(lane >= c0, lane < c0 + 8)
        own = jnp.where(inside, jnp.where(lane == sub + c0, 1.0, 0.0), rows[p])

        def spread_row(v, j):
            return jnp.broadcast_to(v[j : j + 1, :], (8, 128))

        terms = []
        for j in range(8):
            column = zero
            for i in range(j, 8):
                column = jnp.where(sub == i, x[i, j], column)
            terms.append(column * spread_row(own, j))
        u = tree(terms)
        out.append(jnp.where(lane < c0 + 8, u, 0.0))
        if p == 15:
            break
        terms = []
        for j in range(8):
            column = zero
            for i in range(j + 1):
                column = jnp.where(sub == i, x[j, i], column)
            terms.append(column * spread_row(u, j))
        v = tree(terms)
        vs = [spread_row(v, j) for j in range(8)]
        for i in range(p + 1, 16):
            left = [jnp.broadcast_to(rows[i][:, c0 + j : c0 + j + 1], (8, 128)) for j in range(8)]
            rows[i] = jnp.where(inside, 0.0, rows[i]) - tree([a * b for a, b in zip(left, vs)])
    return out


def factor_kernel(a_ref, wh_ref, wl_ref, lh_ref, ll_ref):
    order = a_ref.shape[0]
    for ref in (wh_ref, wl_ref, lh_ref, ll_ref):
        ref[...] = jnp.zeros_like(ref)

    def step(k, carry):
        start = pl.multiple_of(k * NB, NB)
        ks = pl.ds(start, NB)
        strip = (lh_ref[ks, :], ll_ref[ks, :])
        diag = a_ref[ks, ks].astype(F32) - dot3(strip, strip, NT)
        inv = jnp.concatenate(inverse_factor([diag[8 * i : 8 * i + 8, :] for i in range(16)]), axis=0)
        inv = halves(inv)
        c = a_ref[:, ks].astype(F32) - dot3((lh_ref[...], ll_ref[...]), strip, NT)
        low = dot3(halves(c), inv, NT)
        row_id = lax.broadcasted_iota(jnp.int32, (order, NB), 0)
        low = jnp.where(row_id >= start, low, 0.0)
        lh, ll = halves(low)
        col_id = lax.broadcasted_iota(jnp.int32, (NB, order), 1)
        row_of = lax.broadcasted_iota(jnp.int32, (NB, order), 0) + start
        y = jnp.where(col_id == row_of, 1.0, 0.0) - dot3(strip, (wh_ref[...], wl_ref[...]), NN)
        wh, wl = halves(dot3(inv, halves(y), NN))
        lh_ref[:, ks] = lh
        ll_ref[:, ks] = ll
        wh_ref[ks, :] = wh
        wl_ref[ks, :] = wl
        return carry

    lax.fori_loop(0, order // NB, step, 0)


def inverse_cholesky(matrix):
    n = matrix.shape[0]
    shape = jax.ShapeDtypeStruct((n, n), BF16)
    return pl.pallas_call(
        factor_kernel,
        out_shape=(shape, shape),
        in_specs=[pl.BlockSpec(memory_space=pltpu.VMEM)],
        out_specs=(pl.BlockSpec(memory_space=pltpu.VMEM),) * 2,
        scratch_shapes=[pltpu.VMEM((n, n), BF16)] * 2,
        compiler_params=pltpu.CompilerParams(vmem_limit_bytes=48 * 1024 * 1024),
        cost_estimate=pl.CostEstimate(flops=20 * n**3, bytes_accessed=8 * n * n, transcendentals=n),
        name="inverse_cholesky",
    )(matrix)


def on_device(pivot_blocks, couplings, pattern, front_base):
    ncol = lax.axis_size("x") * lax.axis_size("z")
    nlayer = lax.axis_size("y") * lax.axis_size("core")
    col_rank = lax.axis_index(("x", "z"))
    layer_rank = lax.axis_index(("y", "core"))
    rows_dev = couplings.shape[1]
    order = couplings.shape[2]
    total = front_base.shape[1]
    piv_dev = P2 // ncol
    nonpiv = rows_dev - piv_dev
    group = nonpiv // nlayer
    blocks_r = total // BLK
    blocks_c = order // BLK
    width = ncol * group

    def gather(v):
        v = lax.all_gather(v, "z", axis=0, tiled=True)
        return lax.all_gather(v, "x", axis=0, tiled=True)

    row_block = (col_rank * rows_dev + jnp.arange(rows_dev, dtype=jnp.int32)) // BLK
    select = (row_block[:, None] == jnp.arange(blocks_r, dtype=jnp.int32)[None, :]).astype(F32)
    row_mask = jnp.dot(select, pattern[0].astype(F32), preferred_element_type=F32)
    masked = couplings[0].reshape(rows_dev, blocks_c, BLK) * row_mask[:, :, None].astype(BF16)
    masked = masked.reshape(rows_dev, order)
    every = gather(masked).reshape(ncol, rows_dev, order)
    m_piv = every[:, :piv_dev].reshape(P2, order)
    m_rest = every[:, piv_dev:].reshape(ncol, nlayer, group, order)
    m_rest = jnp.transpose(m_rest, (1, 0, 2, 3)).reshape(nlayer * width, order)

    split = front_base.reshape(rows_dev, ncol, rows_dev)
    base_piv = split[:, :, :piv_dev].reshape(rows_dev, P2)
    base_rest = split[piv_dev:, :, piv_dev:].reshape(nonpiv, ncol, nlayer, group)
    base_own = lax.dynamic_index_in_dim(base_rest, layer_rank, 2, keepdims=False)
    base_own = base_own.reshape(nonpiv, width)
    chosen_base = lax.dynamic_slice_in_dim(base_piv, piv_dev + layer_rank * group, group, 0)
    base_every = gather(jnp.concatenate([base_piv[:piv_dev], chosen_base], axis=0))
    base_every = base_every.reshape(ncol, piv_dev + group, P2)
    base_top = base_every[:, :piv_dev].reshape(P2, P2)
    base_chosen = base_every[:, piv_dev:].reshape(width, P2)

    wh, wl = inverse_cholesky(pivot_blocks[0])

    def solve(m):
        return (dot(m, wh, NT) + dot(m, wl, NT)).astype(BF16)

    p_piv = solve(m_piv)
    panel = solve(masked)
    own = panel[piv_dev:]
    layers = ("y", "core")
    update = dot(jnp.concatenate([p_piv, own], axis=0), p_piv, NT).astype(BF16)
    update = lax.psum(update, layers).astype(F32)
    p_rest = solve(m_rest)
    rest = dot(p_rest, p_piv, NT).astype(BF16).reshape(nlayer, width, P2)
    mixed = dot(own, p_rest, NT).astype(BF16).reshape(nonpiv, nlayer, width)
    extra = nonpiv * width // P2
    mixed = jnp.transpose(mixed, (1, 0, 2)).reshape(nlayer, extra, P2)
    both = jnp.concatenate([rest, mixed], axis=1).reshape(nlayer * (width + extra), P2)
    both = lax.psum_scatter(both, layers, scatter_dimension=0, tiled=True).astype(F32)

    w2h, w2l = inverse_cholesky(base_top - update[:P2])
    x_own = base_piv[piv_dev:] - update[P2:]
    x_chosen = base_chosen - both[:width]
    x = jnp.concatenate([x_own, x_chosen], axis=0)
    xh = lax.reduce_precision(x, 8, 7)
    xl = (x - xh).astype(BF16)
    factor = dot3((xh.astype(BF16), xl), (w2h, w2l), NT).astype(BF16)
    factor_rows = factor[:nonpiv]
    schur = base_own - both[width:].reshape(nonpiv, width) - dot(factor_rows, factor[nonpiv:], NT)
    return (panel[None], factor_rows, schur)


def solution(mesh):
    inner = Mesh(mesh.devices.reshape(4, 2, 4, 16), ("y", "core", "x", "z"))
    layer, col = ("y", "core"), ("x", "z")
    in_specs = (P(layer, None, None), P(layer, col, None), P(layer, None, None), P(col, None))
    out_specs = (P(layer, col, None), P(col, None), P(col, layer))
    return jax.shard_map(on_device, mesh=inner, in_specs=in_specs, out_specs=out_specs, check_vma=False)
```

```python
import jax
import jax.numpy as jnp
from jax import lax
from jax.experimental import pallas as pl
from jax.experimental.pallas import tpu as pltpu
from jax.sharding import Mesh, PartitionSpec as P

P2 = 1024
BLK = 256
NB = 128
F32 = jnp.float32
BF16 = jnp.bfloat16
NT = (((1,), (1,)), ((), ()))
NN = (((1,), (0,)), ((), ()))


def halves(x):
    hi = x.astype(BF16)
    return hi, (x - hi.astype(F32)).astype(BF16)


def dot(a, b, dims):
    return lax.dot_general(a, b, dims, preferred_element_type=F32)


def dot3(a, b, dims):
    return dot(a[0], b[0], dims) + dot(a[1], b[0], dims) + dot(a[0], b[1], dims)


def tree(terms):
    while len(terms) > 1:
        terms = [a + b for a, b in zip(terms[::2], terms[1::2])] + terms[len(terms) & ~1 :]
    return terms[0]


def small_factor(row, first):
    spread = [jnp.broadcast_to(row[:, first + j : first + j + 1], (8, 128)) for j in range(8)]
    s = {(i, j): jnp.broadcast_to(spread[j][i : i + 1, :], (8, 128)) for j in range(8) for i in range(j, 8)}
    x, t = {}, {}
    for j in range(8):
        r = lax.rsqrt(s[j, j])
        x[j, j] = r
        for m in range(j):
            x[j, m] = -r * t[j, m]
        low = {i: s[i, j] * r for i in range(j + 1, 8)}
        for m in range(j + 1, 8):
            for i in range(m, 8):
                s[i, m] = s[i, m] - low[i] * low[m]
        for i in range(j + 1, 8):
            for m in range(j + 1):
                term = low[i] * x[j, m]
                t[i, m] = t[i, m] + term if (i, m) in t else term
    return x


def inverse_factor(rows):
    lane = lax.broadcasted_iota(jnp.int32, (8, 128), 1)
    sub = lax.broadcasted_iota(jnp.int32, (8, 128), 0)
    zero = jnp.zeros((8, 128), F32)
    rows = list(rows)
    out = []
    for p in range(16):
        c0 = 8 * p
        x = small_factor(rows[p], c0)
        inside = jnp.logical_and(lane >= c0, lane < c0 + 8)
        own = jnp.where(inside, jnp.where(lane == sub + c0, 1.0, 0.0), rows[p])

        def spread_row(v, j):
            return jnp.broadcast_to(v[j : j + 1, :], (8, 128))

        terms = []
        for j in range(8):
            column = zero
            for i in range(j, 8):
                column = jnp.where(sub == i, x[i, j], column)
            terms.append(column * spread_row(own, j))
        u = tree(terms)
        out.append(jnp.where(lane < c0 + 8, u, 0.0))
        if p == 15:
            break
        terms = []
        for j in range(8):
            column = zero
            for i in range(j + 1):
                column = jnp.where(sub == i, x[j, i], column)
            terms.append(column * spread_row(u, j))
        v = tree(terms)
        vs = [spread_row(v, j) for j in range(8)]
        for i in range(p + 1, 16):
            left = [jnp.broadcast_to(rows[i][:, c0 + j : c0 + j + 1], (8, 128)) for j in range(8)]
            rows[i] = jnp.where(inside, 0.0, rows[i]) - tree([a * b for a, b in zip(left, vs)])
    return out


def factor_kernel(a_ref, wh_ref, wl_ref, lh_ref, ll_ref):
    order = a_ref.shape[0]
    for ref in (wh_ref, wl_ref, lh_ref, ll_ref):
        ref[...] = jnp.zeros_like(ref)

    def step(k, carry):
        start = pl.multiple_of(k * NB, NB)
        ks = pl.ds(start, NB)
        strip = (lh_ref[ks, :], ll_ref[ks, :])
        diag = a_ref[ks, ks].astype(F32) - dot3(strip, strip, NT)
        inv = jnp.concatenate(inverse_factor([diag[8 * i : 8 * i + 8, :] for i in range(16)]), axis=0)
        inv = halves(inv)
        c = a_ref[:, ks].astype(F32) - dot3((lh_ref[...], ll_ref[...]), strip, NT)
        low = dot3(halves(c), inv, NT)
        row_id = lax.broadcasted_iota(jnp.int32, (order, NB), 0)
        low = jnp.where(row_id >= start, low, 0.0)
        lh, ll = halves(low)
        col_id = lax.broadcasted_iota(jnp.int32, (NB, order), 1)
        row_of = lax.broadcasted_iota(jnp.int32, (NB, order), 0) + start
        y = jnp.where(col_id == row_of, 1.0, 0.0) - dot3(strip, (wh_ref[...], wl_ref[...]), NN)
        wh, wl = halves(dot3(inv, halves(y), NN))
        lh_ref[:, ks] = lh
        ll_ref[:, ks] = ll
        wh_ref[ks, :] = wh
        wl_ref[ks, :] = wl
        return carry

    lax.fori_loop(0, order // NB, step, 0)


def inverse_cholesky(matrix):
    n = matrix.shape[0]
    shape = jax.ShapeDtypeStruct((n, n), BF16)
    return pl.pallas_call(
        factor_kernel,
        out_shape=(shape, shape),
        in_specs=[pl.BlockSpec(memory_space=pltpu.VMEM)],
        out_specs=(pl.BlockSpec(memory_space=pltpu.VMEM),) * 2,
        scratch_shapes=[pltpu.VMEM((n, n), BF16)] * 2,
        compiler_params=pltpu.CompilerParams(vmem_limit_bytes=48 * 1024 * 1024),
        cost_estimate=pl.CostEstimate(flops=20 * n**3, bytes_accessed=8 * n * n, transcendentals=n),
        name="inverse_cholesky",
    )(matrix)


def on_device(pivot_blocks, couplings, pattern, front_base):
    ncol = lax.axis_size("x") * lax.axis_size("z")
    nlayer = lax.axis_size("y") * lax.axis_size("core")
    col_rank = lax.axis_index(("x", "z"))
    layer_rank = lax.axis_index(("y", "core"))
    rows_dev = couplings.shape[1]
    order = couplings.shape[2]
    total = front_base.shape[1]
    piv_dev = P2 // ncol
    nonpiv = rows_dev - piv_dev
    group = nonpiv // nlayer
    blocks_r = total // BLK
    blocks_c = order // BLK
    width = ncol * group

    row_block = (col_rank * rows_dev + jnp.arange(rows_dev, dtype=jnp.int32)) // BLK
    select = (row_block[:, None] == jnp.arange(blocks_r, dtype=jnp.int32)[None, :]).astype(F32)
    row_mask = jnp.dot(select, pattern[0].astype(F32), preferred_element_type=F32)
    masked = couplings[0].reshape(rows_dev, blocks_c, BLK) * row_mask[:, :, None].astype(BF16)
    masked = masked.reshape(rows_dev, order)
    split = front_base.reshape(rows_dev, ncol, rows_dev)
    base_piv = split[:, :, :piv_dev].reshape(rows_dev, P2)
    base_rest = split[piv_dev:, :, piv_dev:].reshape(nonpiv, ncol, nlayer, group)
    base_own = lax.dynamic_index_in_dim(base_rest, layer_rank, 2, keepdims=False)
    base_own = base_own.reshape(nonpiv, width)
    chosen_base = lax.dynamic_slice_in_dim(base_piv, piv_dev + layer_rank * group, group, 0)

    sent = lax.all_gather(masked, "x", axis=0)
    base_sent = lax.all_gather(base_piv[:piv_dev], "x", axis=0)
    chosen_sent = lax.all_gather(chosen_base, "x", axis=0)
    held = (pivot_blocks[0], sent, base_sent, chosen_sent)
    pivot, sent, base_sent, chosen_sent = lax.optimization_barrier(held)
    every = lax.all_gather(sent, "z", axis=0)
    base_every = lax.all_gather(base_sent, "z", axis=0)

    wh, wl = inverse_cholesky(pivot)

    def solve(m):
        return (dot(m, wh, NT) + dot(m, wl, NT)).astype(BF16)

    p_piv = solve(jnp.swapaxes(every[:, :, :piv_dev], 0, 1).reshape(P2, order))
    panel = solve(masked)
    own = panel[piv_dev:]
    layers = ("y", "core")
    spare = jnp.zeros((4 * nonpiv - own.shape[0], order), BF16)
    update = dot(jnp.concatenate([p_piv, own, spare], axis=0), p_piv, NT).astype(BF16)
    update, every, base_every = lax.optimization_barrier((update, every, base_every))
    base_top = jnp.swapaxes(base_every, 0, 1).reshape(P2, P2)
    update = lax.psum_scatter(update, layers, scatter_dimension=0, tiled=True)
    m_rest = every[:, :, piv_dev:].reshape(*every.shape[:2], nlayer, group, order)
    m_rest = jnp.transpose(m_rest, (2, 1, 0, 3, 4)).reshape(nlayer * width, order)
    p_rest = solve(m_rest)
    update, p_rest = lax.optimization_barrier((update, p_rest))
    update = lax.all_gather(update, layers, axis=0, tiled=True)
    rest = dot(p_rest, p_piv, NT).astype(BF16).reshape(nlayer, width, P2)
    mixed = dot(own, p_rest, NT).astype(BF16).reshape(nonpiv, nlayer, width)
    extra = nonpiv * width // P2
    mixed = jnp.transpose(mixed, (1, 0, 2)).reshape(nlayer, extra, P2)
    both = jnp.concatenate([rest, mixed], axis=1).reshape(nlayer * (width + extra), P2)
    update, both, chosen_sent = lax.optimization_barrier((update, both, chosen_sent))
    base_chosen = lax.all_gather(chosen_sent, "z", axis=0)
    update = update.astype(F32)
    both = lax.psum_scatter(both, layers, scatter_dimension=0, tiled=True)

    w2h, w2l = inverse_cholesky(base_top - update[:P2])
    w2h, both, base_chosen = lax.optimization_barrier((w2h, both, base_chosen))
    both = both.astype(F32)
    base_chosen = jnp.swapaxes(base_chosen, 0, 1).reshape(width, P2)
    x_own = base_piv[piv_dev:] - update[P2 : P2 + nonpiv]
    x_chosen = base_chosen - both[:width]
    x = jnp.concatenate([x_own, x_chosen], axis=0)
    xh = lax.reduce_precision(x, 8, 7)
    xl = (x - xh).astype(BF16)
    factor = dot3((xh.astype(BF16), xl), (w2h, w2l), NT).astype(BF16)
    factor_rows = factor[:nonpiv]
    schur = base_own - both[width:].reshape(nonpiv, width) - dot(factor_rows, factor[nonpiv:], NT)
    return (panel[None], factor_rows, schur)


def solution(mesh):
    inner = Mesh(mesh.devices.reshape(4, 2, 4, 16), ("y", "core", "x", "z"))
    layer, col = ("y", "core"), ("x", "z")
    in_specs = (P(layer, None, None), P(layer, col, None), P(layer, None, None), P(col, None))
    out_specs = (P(layer, col, None), P(col, None), P(col, layer))
    return jax.shard_map(on_device, mesh=inner, in_specs=in_specs, out_specs=out_specs, check_vma=False)
```

```python
import jax
import jax.numpy as jnp
from jax import lax
from jax.experimental import pallas as pl
from jax.experimental.pallas import tpu as pltpu
from jax.sharding import Mesh, PartitionSpec as P

P2 = 1024
BLK = 256
NB = 128
F32 = jnp.float32
BF16 = jnp.bfloat16
NT = (((1,), (1,)), ((), ()))
NN = (((1,), (0,)), ((), ()))


def halves(x):
    hi = x.astype(BF16)
    return hi, (x - hi.astype(F32)).astype(BF16)


def thirds(x):
    hi = lax.reduce_precision(x, 8, 7)
    rest = x - hi
    mid = lax.reduce_precision(rest, 8, 7)
    return hi.astype(BF16), mid.astype(BF16), (rest - mid).astype(BF16)


def dot(a, b, dims):
    return lax.dot_general(a, b, dims, preferred_element_type=F32)


def dot3(a, b, dims):
    return dot(a[0], b[0], dims) + dot(a[1], b[0], dims) + dot(a[0], b[1], dims)


def tree(terms):
    while len(terms) > 1:
        terms = [a + b for a, b in zip(terms[::2], terms[1::2])] + terms[len(terms) & ~1 :]
    return terms[0]


def small_factor(row, first):
    spread = [jnp.broadcast_to(row[:, first + j : first + j + 1], (8, 128)) for j in range(8)]
    s = {(i, j): jnp.broadcast_to(spread[j][i : i + 1, :], (8, 128)) for j in range(8) for i in range(j, 8)}
    x, t = {}, {}
    for j in range(8):
        r = lax.rsqrt(s[j, j])
        x[j, j] = r
        for m in range(j):
            x[j, m] = -r * t[j, m]
        low = {i: s[i, j] * r for i in range(j + 1, 8)}
        for m in range(j + 1, 8):
            for i in range(m, 8):
                s[i, m] = s[i, m] - low[i] * low[m]
        for i in range(j + 1, 8):
            for m in range(j + 1):
                term = low[i] * x[j, m]
                t[i, m] = t[i, m] + term if (i, m) in t else term
    return x


def inverse_factor(rows):
    lane = lax.broadcasted_iota(jnp.int32, (8, 128), 1)
    sub = lax.broadcasted_iota(jnp.int32, (8, 128), 0)
    zero = jnp.zeros((8, 128), F32)
    rows = list(rows)
    out = []
    for p in range(16):
        c0 = 8 * p
        x = small_factor(rows[p], c0)
        inside = jnp.logical_and(lane >= c0, lane < c0 + 8)
        own = jnp.where(inside, jnp.where(lane == sub + c0, 1.0, 0.0), rows[p])

        def spread_row(v, j):
            return jnp.broadcast_to(v[j : j + 1, :], (8, 128))

        terms = []
        for j in range(8):
            column = zero
            for i in range(j, 8):
                column = jnp.where(sub == i, x[i, j], column)
            terms.append(column * spread_row(own, j))
        u = tree(terms)
        out.append(jnp.where(lane < c0 + 8, u, 0.0))
        if p == 15:
            break
        terms = []
        for j in range(8):
            column = zero
            for i in range(j + 1):
                column = jnp.where(sub == i, x[j, i], column)
            terms.append(column * spread_row(u, j))
        v = tree(terms)
        vs = [spread_row(v, j) for j in range(8)]
        for i in range(p + 1, 16):
            left = [jnp.broadcast_to(rows[i][:, c0 + j : c0 + j + 1], (8, 128)) for j in range(8)]
            rows[i] = jnp.where(inside, 0.0, rows[i]) - tree([a * b for a, b in zip(left, vs)])
    return out


def factor_kernel(a_ref, wh_ref, wl_ref, lh_ref, ll_ref):
    order = a_ref.shape[0]
    for ref in (wh_ref, wl_ref, lh_ref, ll_ref):
        ref[...] = jnp.zeros_like(ref)

    def step(k, carry):
        start = pl.multiple_of(k * NB, NB)
        ks = pl.ds(start, NB)
        strip = (lh_ref[ks, :], ll_ref[ks, :])
        diag = a_ref[ks, ks].astype(F32) - dot3(strip, strip, NT)
        inv = jnp.concatenate(inverse_factor([diag[8 * i : 8 * i + 8, :] for i in range(16)]), axis=0)
        inv = halves(inv)
        c = a_ref[:, ks].astype(F32) - dot3((lh_ref[...], ll_ref[...]), strip, NT)
        low = dot3(halves(c), inv, NT)
        row_id = lax.broadcasted_iota(jnp.int32, (order, NB), 0)
        low = jnp.where(row_id >= start, low, 0.0)
        lh, ll = halves(low)
        col_id = lax.broadcasted_iota(jnp.int32, (NB, order), 1)
        row_of = lax.broadcasted_iota(jnp.int32, (NB, order), 0) + start
        y = jnp.where(col_id == row_of, 1.0, 0.0) - dot3(strip, (wh_ref[...], wl_ref[...]), NN)
        wh, wl = halves(dot3(inv, halves(y), NN))
        lh_ref[:, ks] = lh
        ll_ref[:, ks] = ll
        wh_ref[ks, :] = wh
        wl_ref[ks, :] = wl
        return carry

    lax.fori_loop(0, order // NB, step, 0)


def inverse_cholesky(matrix):
    n = matrix.shape[0]
    shape = jax.ShapeDtypeStruct((n, n), BF16)
    return pl.pallas_call(
        factor_kernel,
        out_shape=(shape, shape),
        in_specs=[pl.BlockSpec(memory_space=pltpu.VMEM)],
        out_specs=(pl.BlockSpec(memory_space=pltpu.VMEM),) * 2,
        scratch_shapes=[pltpu.VMEM((n, n), BF16)] * 2,
        compiler_params=pltpu.CompilerParams(vmem_limit_bytes=48 * 1024 * 1024),
        cost_estimate=pl.CostEstimate(flops=20 * n**3, bytes_accessed=8 * n * n, transcendentals=n),
        name="inverse_cholesky",
    )(matrix)


def on_device(pivot_blocks, couplings, pattern, front_base):
    ncol = lax.axis_size("x") * lax.axis_size("z")
    nlayer = lax.axis_size("y") * lax.axis_size("core")
    col_rank = lax.axis_index(("x", "z"))
    layer_rank = lax.axis_index(("y", "core"))
    rows_dev = couplings.shape[1]
    order = couplings.shape[2]
    total = front_base.shape[1]
    piv_dev = P2 // ncol
    nonpiv = rows_dev - piv_dev
    group = nonpiv // nlayer
    blocks_r = total // BLK
    blocks_c = order // BLK
    width = ncol * group

    row_block = (col_rank * rows_dev + jnp.arange(rows_dev, dtype=jnp.int32)) // BLK
    select = (row_block[:, None] == jnp.arange(blocks_r, dtype=jnp.int32)[None, :]).astype(F32)
    row_mask = jnp.dot(select, pattern[0].astype(F32), preferred_element_type=F32)
    masked = couplings[0].reshape(rows_dev, blocks_c, BLK) * row_mask[:, :, None].astype(BF16)
    masked = masked.reshape(rows_dev, order)
    split = front_base.reshape(rows_dev, ncol, rows_dev)
    base_piv = split[:, :, :piv_dev].reshape(rows_dev, P2)
    base_rest = split[piv_dev:, :, piv_dev:].reshape(nonpiv, ncol, nlayer, group)
    base_own = lax.dynamic_index_in_dim(base_rest, layer_rank, 2, keepdims=False)
    base_own = base_own.reshape(nonpiv, width)
    chosen_base = lax.dynamic_slice_in_dim(base_piv, piv_dev + layer_rank * group, group, 0)

    sent = jnp.concatenate([masked, *thirds(base_piv[:piv_dev]), *thirds(chosen_base)], axis=0)
    sent = lax.all_gather(sent, "x", axis=0)
    pivot, sent = lax.optimization_barrier((pivot_blocks[0], sent))
    every = lax.all_gather(sent, "z", axis=0)

    wh, wl = inverse_cholesky(pivot)

    def solve(m):
        return (dot(m, wh, NT) + dot(m, wl, NT)).astype(BF16)

    p_piv = solve(jnp.swapaxes(every[:, :, :piv_dev], 0, 1).reshape(P2, order))
    panel = solve(masked)
    own = panel[piv_dev:]
    layers = ("y", "core")
    spare = jnp.zeros((4 * nonpiv - own.shape[0], order), BF16)
    update = dot(jnp.concatenate([p_piv, own, spare], axis=0), p_piv, NT).astype(BF16)
    update, every = lax.optimization_barrier((update, every))

    def joined(first, count):
        hi, mid, lo = (every[:, :, first + i * count : first + (i + 1) * count].astype(F32) for i in range(3))
        return jnp.swapaxes(hi + mid + lo, 0, 1).reshape(ncol * count, P2)

    base_top = joined(rows_dev, piv_dev)
    base_chosen = joined(rows_dev + 3 * piv_dev, group)
    update = lax.psum_scatter(update, layers, scatter_dimension=0, tiled=True)
    m_rest = every[:, :, piv_dev:rows_dev].reshape(*every.shape[:2], nlayer, group, order)
    m_rest = jnp.transpose(m_rest, (2, 1, 0, 3, 4)).reshape(nlayer * width, order)
    p_rest = solve(m_rest)
    update, p_rest = lax.optimization_barrier((update, p_rest))
    update = lax.all_gather(update, layers, axis=0, tiled=True)
    rest = dot(p_rest, p_piv, NT).astype(BF16).reshape(nlayer, width, P2)
    mixed = dot(own, p_rest, NT).astype(BF16).reshape(nonpiv, nlayer, width)
    extra = nonpiv * width // P2
    mixed = jnp.transpose(mixed, (1, 0, 2)).reshape(nlayer, extra, P2)
    both = jnp.concatenate([rest, mixed], axis=1).reshape(nlayer * (width + extra), P2)
    held = (update, both, base_top, base_chosen, base_own, base_piv[piv_dev:])
    update, both, base_top, base_chosen, base_own, base_rows = lax.optimization_barrier(held)
    update = update.astype(F32)
    both = lax.psum_scatter(both, layers, scatter_dimension=0, tiled=True)

    w2h, w2l = inverse_cholesky(base_top - update[:P2])
    w2h, both = lax.optimization_barrier((w2h, both))
    both = both.astype(F32)
    x_own = base_rows - update[P2 : P2 + nonpiv]
    x_chosen = base_chosen - both[:width]
    x = jnp.concatenate([x_own, x_chosen], axis=0)
    xh = lax.reduce_precision(x, 8, 7)
    xl = (x - xh).astype(BF16)
    factor = dot3((xh.astype(BF16), xl), (w2h, w2l), NT).astype(BF16)
    factor_rows = factor[:nonpiv]
    schur = base_own - both[width:].reshape(nonpiv, width) - dot(factor_rows, factor[nonpiv:], NT)
    return (panel[None], factor_rows, schur)


def solution(mesh):
    inner = Mesh(mesh.devices.reshape(4, 2, 4, 16), ("y", "core", "x", "z"))
    layer, col = ("y", "core"), ("x", "z")
    in_specs = (P(layer, None, None), P(layer, col, None), P(layer, None, None), P(col, None))
    out_specs = (P(layer, col, None), P(col, None), P(col, layer))
    return jax.shard_map(on_device, mesh=inner, in_specs=in_specs, out_specs=out_specs, check_vma=False)
```
